32 devices in a mesh: head: 4 (over y, x), batch: 8 (over z, core).
Axes of the slice: x: 2, y: 2, z: 4, core: 2. Of those that a mesh axis runs over, the one named last changes fastest.
Arguments:
- hidden_in: bfloat16 [8, 256, 4096], P('batch', None, 'head')
- w_query: bfloat16 [4096, 4096], P('batch', 'head'), may hold values from -0.09375 to 0.09375
- w_key: bfloat16 [4096, 4096], P('batch', 'head'), may hold values from -0.09375 to 0.09375
- w_value: bfloat16 [4096, 4096], P('batch', 'head'), may hold values from -0.09375 to 0.09375
- w_beta: bfloat16 [4096, 32], P('batch', 'head'), may hold values from -0.09375 to 0.09375
- w_out: bfloat16 [4096, 4096], P('head', 'batch'), may hold values from -0.125 to 0.125
- mem_pos: int32 [8, 2, 64], P('batch'), may hold values from 0 to 127, as said below
- memory_in: float32 [8, 32, 128, 128], P('batch', 'head'), may hold values from -6 to 6
Outputs:
- hidden_out: bfloat16 [8, 256, 4096], P('batch', None, 'head')
- memory_out: float32 [8, 32, 128, 128], P('batch', 'head')
The draws below stay inside these ranges and needn't reach their ends.
Inputs may be any that keep to these rules, and one draw needn't show every extreme that they name: `mem_pos`: within each sequence and segment the 64 positions are distinct and ascending.
All inputs are finite; a program needn't handle non-finite values.
Results may differ from the reference program's by a relative error of at most 0.005.
Values may be sent and summed in bfloat16 or wider, within the bound.
No kernel may reach another device: no remote copies, remote signals or barrier semaphores. Data moves between devices by JAX's collectives and lax.ppermute only.
A program may use at most 128 MiB of HBM per device.

```python
import jax
import jax.numpy as jnp
from jax import lax

D = 4096
HEADS = 32
DH = 128
SEGS = 2
MEM = 64
SEG_LEN = 128
ROWS = 256
BATCH = 8


def draw_hidden_in(key, part):
    columns = jnp.arange(D, dtype=jnp.float32) / D
    rising = 0.6 * jnp.power(3.0, columns)
    values = jax.random.normal(key, (BATCH, ROWS, D), jnp.float32) * rising
    return values.astype(jnp.bfloat16)


def draw_mem_pos(key, part):
    keys = jax.random.split(jax.random.fold_in(key, 7), BATCH * SEGS)
    orders = jax.vmap(lambda single: jax.random.permutation(single, SEG_LEN))(keys)
    chosen = jnp.sort(orders[:, :MEM], axis=-1)
    return chosen.reshape(BATCH, SEGS, MEM).astype(jnp.int32)


def spiked(entries, rng, source, target, parts, factor):
    def block_of(dim):
        return (jnp.arange(entries.shape[dim]) // (entries.shape[dim] // parts)).reshape((-1,) + (1,) * (entries.ndim - 1 - dim))

    near = jax.random.permutation(rng, parts)[block_of(target)]
    second = (block_of(target) + parts // 2) % parts
    return jnp.where((block_of(source) == near) | (block_of(source) == second), factor * entries, entries)


def block_levels(own_key, shape, cuts, least, largest):
    def one(dim, blocks):
        steps = jax.random.uniform(jax.random.fold_in(jax.random.fold_in(own_key, 6), dim), (blocks,), jnp.float32, least / len(cuts), largest / len(cuts))
        return jnp.repeat(jnp.exp(steps), shape[dim] // blocks).reshape((-1,) + (1,) * (len(shape) - dim - 1))

    gain = one(*cuts[0])
    for cut in cuts[1:]:
        gain = gain * one(*cut)
    return gain


def gaussian(key, shape, deviation, bound, cuts=(), kind=jnp.bfloat16):
    level = block_levels(key, shape, cuts, -0.22, 0.18) if cuts else 1.0
    drawn = jax.random.normal(key, shape, jnp.float32) * deviation * level
    return jnp.minimum(jnp.maximum(drawn, -bound), bound).astype(kind)


def bell_draw_with(rng, extent, spread, most, pieces, heavy, held_as=jnp.bfloat16):
    values = spread * jax.random.normal(rng, extent, jnp.float32)
    if pieces:
        values = values * block_levels(rng, extent, pieces, -0.22, 0.18)
    return jnp.clip(spiked(values, jax.random.fold_in(rng, 3), *heavy), -most, most).astype(held_as)


def setup_inputs(seed: int = 0) -> dict:
    key_of = jax.random.split(jax.random.key(seed), 9)
    hidden_in = draw_hidden_in(jax.random.fold_in(key_of[8], 71), 0)
    w_query = gaussian(key_of[1], (D, HEADS * DH), D ** -0.5, 0.09375, ((0, 8), (1, 4)))
    w_key = gaussian(key_of[2], (D, HEADS * DH), D ** -0.5, 0.09375, ((0, 8), (1, 4)))
    w_value = gaussian(key_of[3], (D, HEADS * DH), D ** -0.5, 0.09375, ((0, 8), (1, 4)))
    w_beta = gaussian(key_of[4], (D, HEADS), D ** -0.5, 0.09375, ((0, 8), (1, 4)))
    w_out = bell_draw_with(key_of[5], (HEADS * DH, D), (HEADS * DH) ** -0.5, 0.125, ((0, 4), (1, 8)), (0, 1, 8, 2.0))
    mem_pos = draw_mem_pos(jax.random.fold_in(key_of[8], 71), 0)
    memory_in = gaussian(key_of[7], (BATCH, HEADS, DH, DH), 1.0, 6.0, ((0, 8), (1, 4)), jnp.float32)
    return dict(hidden_in=hidden_in, w_query=w_query, w_key=w_key, w_value=w_value, w_beta=w_beta, w_out=w_out, mem_pos=mem_pos, memory_in=memory_in)


epsilon = 1e-05

def recur(query, keys, values, beta, state):
    highest = lax.Precision.HIGHEST
    readouts = []
    for segment in range(query.shape[1]):
        readouts.append(jnp.einsum('bhij,blhj->blhi', state, query[:, segment], precision=highest).astype(jnp.bfloat16))
        recalled = jnp.einsum('bhij,bmhj->bmhi', state, keys[:, segment], precision=highest)
        change = beta[:, segment][..., None] * (values[:, segment] - recalled)
        state = state + jnp.einsum('bmhi,bmhj->bhij', change, keys[:, segment], precision=highest)
    return (jnp.stack(readouts, axis=1), state)

def reference(hidden_in, w_query, w_key, w_value, w_beta, w_out, mem_pos, memory_in):
    x_float = hidden_in.astype(jnp.float32)
    mean_square = lax.optimization_barrier(jnp.mean(x_float * x_float, axis=2, keepdims=True))
    normed = (x_float * lax.rsqrt(mean_square + epsilon)).astype(jnp.bfloat16)
    token_rows = normed.reshape(BATCH * ROWS, D)
    query = jnp.dot(token_rows, w_query, preferred_element_type=jnp.float32) * DH ** (-0.5)
    query = query.reshape(BATCH, SEGS, SEG_LEN, HEADS, DH)
    offsets = (jnp.arange(SEGS, dtype=jnp.int32) * SEG_LEN)[None, :, None]
    picked = (mem_pos + offsets).reshape(BATCH, SEGS * MEM).astype(jnp.int32)
    memory_rows = jax.vmap(lambda block, where: jnp.take(block, where, axis=0))(normed, picked)
    memory_rows = memory_rows.reshape(BATCH * SEGS * MEM, D)
    keys = jnp.dot(memory_rows, w_key, preferred_element_type=jnp.float32).reshape(BATCH, SEGS, MEM, HEADS, DH)
    keys = keys * lax.rsqrt(lax.optimization_barrier(jnp.sum(keys * keys, axis=-1, keepdims=True)) + 1e-06)
    values = jnp.dot(memory_rows, w_value, preferred_element_type=jnp.float32).reshape(BATCH, SEGS, MEM, HEADS, DH)
    beta = jax.nn.sigmoid(jnp.dot(memory_rows, w_beta, preferred_element_type=jnp.float32)).reshape(BATCH, SEGS, MEM, HEADS)
    readout, state = recur(query, keys, values, beta, memory_in)
    readout = readout.reshape(BATCH * ROWS, HEADS * DH)
    mixed = jnp.dot(readout, w_out, preferred_element_type=jnp.float32)
    hidden_out = (mixed + x_float.reshape(BATCH * ROWS, D)).astype(jnp.bfloat16).reshape(BATCH, ROWS, D)
    return (hidden_out, state)
```

```python
import functools

import jax
import jax.numpy as jnp
from jax import lax
from jax.experimental import pallas as pl
from jax.experimental.pallas import tpu as pltpu
from jax.sharding import PartitionSpec as P

SEGS = 2
CORES = 2
epsilon = 1e-05


def recur(query, keys, values, beta, state):
    highest = lax.Precision.HIGHEST
    readouts = []
    for segment in range(query.shape[1]):
        readouts.append(
            jnp.einsum("bhij,blhj->blhi", state, query[:, segment], precision=highest).astype(
                jnp.bfloat16
            )
        )
        recalled = jnp.einsum("bhij,bmhj->bmhi", state, keys[:, segment], precision=highest)
        change = beta[:, segment][..., None] * (values[:, segment] - recalled)
        state = state + jnp.einsum("bmhi,bmhj->bhij", change, keys[:, segment], precision=highest)
    return (jnp.stack(readouts, axis=1), state)


def general_body(hidden_in, w_query, w_key, w_value, w_beta, w_out, mem_pos, memory_in):
    seq_count, row_count, local_width = hidden_in.shape
    seg_rows = row_count // SEGS
    mem_count = mem_pos.shape[2]
    local_heads = w_beta.shape[1]
    local_features = w_query.shape[1]
    head_size = local_features // local_heads
    x_float = hidden_in.astype(jnp.float32)
    whole = lax.all_gather(hidden_in, "head", axis=2, tiled=True)
    whole_float = whole.astype(jnp.float32)
    mean_square = jnp.mean(whole_float * whole_float, axis=2, keepdims=True)
    normed = (whole_float * lax.rsqrt(mean_square + epsilon)).astype(jnp.bfloat16)
    full_width = normed.shape[2]
    offsets = (jnp.arange(SEGS, dtype=jnp.int32) * seg_rows)[None, :, None]
    picked = (mem_pos + offsets).reshape(seq_count, SEGS * mem_count)
    memory_rows = jax.vmap(lambda block, where: jnp.take(block, where, axis=0))(normed, picked)
    memory_rows = memory_rows.reshape(seq_count * SEGS * mem_count, full_width)
    token_rows = normed.reshape(seq_count * row_count, full_width)
    piece_query = lax.all_gather(w_query, "batch", axis=0, tiled=True)
    piece_key = lax.all_gather(w_key, "batch", axis=0, tiled=True)
    piece_value = lax.all_gather(w_value, "batch", axis=0, tiled=True)
    piece_beta = lax.all_gather(w_beta, "batch", axis=0, tiled=True)
    query = jnp.dot(token_rows, piece_query, preferred_element_type=jnp.float32)
    keys = jnp.dot(memory_rows, piece_key, preferred_element_type=jnp.float32)
    values = jnp.dot(memory_rows, piece_value, preferred_element_type=jnp.float32)
    logits = jnp.dot(memory_rows, piece_beta, preferred_element_type=jnp.float32)
    query = (query * head_size ** (-0.5)).reshape(seq_count, SEGS, seg_rows, local_heads, head_size)
    keys = keys.reshape(seq_count, SEGS, mem_count, local_heads, head_size)
    keys = keys * lax.rsqrt(jnp.sum(keys * keys, axis=-1, keepdims=True) + 1e-06)
    values = values.reshape(seq_count, SEGS, mem_count, local_heads, head_size)
    beta = jax.nn.sigmoid(logits).reshape(seq_count, SEGS, mem_count, local_heads)
    readout, state = recur(query, keys, values, beta, memory_in)
    readout = readout.reshape(seq_count * row_count, local_features)
    terms = jnp.dot(
        readout,
        lax.all_gather(w_out, "batch", axis=1, tiled=True),
        preferred_element_type=jnp.float32,
    )
    mixed = lax.psum_scatter(terms, "head", scatter_dimension=1, tiled=True)
    hidden_out = (mixed + x_float.reshape(seq_count * row_count, local_width)).astype(jnp.bfloat16)
    return (hidden_out.reshape(hidden_in.shape), state)


VM = pl.BlockSpec(memory_space=pltpu.VMEM)
SM = pl.BlockSpec(memory_space=pltpu.SMEM)


def call(kernel, args, outs, scratch=(), flops=0, name=None):
    scalars = args[0]
    size = sum(a.size * a.dtype.itemsize for a in list(args[1:]) + list(outs))
    return pl.pallas_call(
        kernel,
        out_shape=outs,
        in_specs=[SM] + [VM] * (len(args) - 1),
        out_specs=[VM] * len(outs),
        scratch_shapes=list(scratch),
        cost_estimate=pl.CostEstimate(flops=flops, bytes_accessed=size, transcendentals=0),
        name=name,
    )(*args)


def norm_kernel(heads, width, ids, *refs):
    blocks = refs[:heads]
    outs = refs[heads:-1]
    held = refs[-1]
    square = None
    for block in blocks:
        value = block[...].astype(jnp.float32)
        part = jnp.sum(value * value, axis=-1, keepdims=True)
        square = part if square is None else square + part
    scale = lax.rsqrt(square / width + epsilon)
    for m, block in enumerate(blocks):
        held[m] = (block[...].astype(jnp.float32) * scale).astype(jnp.bfloat16)
    mix = ids[0] ^ ids[1]
    for s in range(SEGS):
        for j in range(heads):
            outs[s * heads + j][...] = held[mix ^ j, s]


def project_kernel(heads, seg, mem, tile, ids, *refs):
    pieces = refs[:heads]
    pos = refs[heads : 2 * heads]
    own = refs[2 * heads : 2 * heads + 4]
    other = refs[2 * heads + 4 : 2 * heads + 8]
    outs = refs[2 * heads + 8 : 3 * heads + 8]
    rows, picked = refs[3 * heads + 8 :]
    piece = pieces[0].shape[1]
    seg_rows = piece * heads
    mem_rows = pos[0].shape[1]
    for m in range(heads):
        start = pl.multiple_of((ids[0] ^ m) * piece, piece)
        for j in range(heads):
            rows[j, pl.ds(start, piece), :] = pieces[m][j]
    token = lax.broadcasted_iota(jnp.int32, (seg_rows, mem_rows), 0)
    for j in range(heads):
        hot = jnp.where(token == pos[j][seg : seg + 1, :], 1.0, 0.0).astype(jnp.bfloat16)
        picked[j] = lax.dot_general(
            hot, rows[j], (((0,), (0,)), ((), ())), preferred_element_type=jnp.float32
        ).astype(jnp.bfloat16)
    depth = own[0].shape[0]
    mine = pl.ds(pl.multiple_of(ids[2] * depth, depth), depth)
    theirs = pl.ds(pl.multiple_of((1 - ids[2]) * depth, depth), depth)
    flat = lambda ref, part: ref[:, :, part].reshape(-1, depth)

    def product(source, weight, columns):
        return jnp.dot(
            flat(source, mine), own[weight][:, columns], preferred_element_type=jnp.float32
        ) + jnp.dot(
            flat(source, theirs), other[weight][:, columns], preferred_element_type=jnp.float32
        )

    def step(n, carry):
        columns = pl.ds(pl.multiple_of(n * tile, tile), tile)
        for weight, source, top, count in (
            (0, rows, 0, seg_rows),
            (1, picked, seg_rows, mem_rows),
            (2, picked, seg_rows + mem_rows, mem_rows),
        ):
            result = product(source, weight, columns).astype(jnp.bfloat16)
            for j in range(heads):
                outs[j][top : top + count, columns] = result[j * count : (j + 1) * count]
        return carry

    lax.fori_loop(0, own[0].shape[1] // tile, step, 0)
    local_heads = own[3].shape[1]
    contract = (((0,), (1,)), ((), ()))
    for j in range(heads):
        logit = lax.dot_general(
            own[3][...], picked[j, :, mine], contract, preferred_element_type=jnp.float32
        ) + lax.dot_general(
            other[3][...], picked[j, :, theirs], contract, preferred_element_type=jnp.float32
        )
        top = seg_rows + 2 * mem_rows
        outs[j][top:, :mem_rows] = logit.astype(jnp.bfloat16)
        outs[j][top:, mem_rows:] = jnp.zeros(
            (local_heads, outs[j].shape[1] - mem_rows), jnp.bfloat16
        )


def recur_kernel(count, seg_rows, mem_rows, local_heads, ids, *refs):
    parts = refs[:count]
    state_in, readout, state_out = refs[count:]
    size = state_in.shape[-1]
    highest = lax.Precision.HIGHEST

    def total(rows, columns):
        value = parts[0][rows, columns].astype(jnp.float32)
        for part in parts[1:]:
            value = value + part[rows, columns].astype(jnp.float32)
        return value

    top = seg_rows + 2 * mem_rows
    logits = total(slice(top, top + local_heads), slice(0, mem_rows))
    beta = jax.nn.sigmoid(logits).T
    for head in range(local_heads):
        columns = slice(head * size, (head + 1) * size)
        state = state_in[head]
        query = total(slice(0, seg_rows), columns) * size ** (-0.5)
        keys = total(slice(seg_rows, seg_rows + mem_rows), columns)
        values = total(slice(seg_rows + mem_rows, top), columns)
        keys = keys * lax.rsqrt(jnp.sum(keys * keys, axis=-1, keepdims=True) + 1e-06)
        across = (((1,), (1,)), ((), ()))
        readout[:, columns] = lax.dot_general(
            query, state, across, precision=highest, preferred_element_type=jnp.float32
        ).astype(jnp.bfloat16)
        recalled = lax.dot_general(
            keys, state, across, precision=highest, preferred_element_type=jnp.float32
        )
        change = beta[:, head : head + 1] * (values - recalled)
        state_out[head] = state + lax.dot_general(
            change,
            keys,
            (((0,), (0,)), ((), ())),
            precision=highest,
            preferred_element_type=jnp.float32,
        )


def out_kernel(heads, ids, *refs):
    readout = refs[0]
    own = refs[1 : 1 + heads]
    other = refs[1 + heads : 1 + 2 * heads]
    outs = refs[1 + 2 * heads : 1 + 3 * heads]
    held = refs[-1]
    width = own[0].shape[1]
    mix = ids[0] ^ ids[1]
    rows = readout[...]
    for j in range(heads):
        for core, weights in ((ids[2], own[j]), (1 - ids[2], other[j])):
            columns = pl.ds(pl.multiple_of(core * width, width), width)
            held[mix ^ j, :, columns] = jnp.dot(
                rows, weights[...], preferred_element_type=jnp.float32
            )
    for m in range(heads):
        outs[m][...] = held[m].astype(outs[m].dtype)


def line_body(planes, heads, *arrays):
    hidden_in, w_query, w_key, w_value, w_beta, w_out, mem_pos, memory_in = arrays
    row_count, width = hidden_in.shape[1:]
    seg_rows, mem_rows = row_count // SEGS, mem_pos.shape[2]
    piece = seg_rows // heads
    local_heads = w_beta.shape[1]
    features = w_query.shape[1]
    full_width = width * heads
    bf16, f32 = jnp.bfloat16, jnp.float32
    h, b = lax.axis_index("head"), lax.axis_index("batch")
    z, core = b // CORES, b % CORES
    ids = jnp.stack([h, z, core]).astype(jnp.int32)
    shape = jax.ShapeDtypeStruct

    def over_head(value, m):
        return lax.ppermute(value, "head", [(i, i ^ m) for i in range(heads)])

    def over_z(value, j):
        return lax.ppermute(
            value, "batch", [(i, i ^ (j * CORES)) for i in range(planes * CORES)]
        )

    def over_core(value):
        return lax.ppermute(value, "batch", [(i, i ^ 1) for i in range(planes * CORES)])

    def edge(value, i):
        pairs = []
        for c in range(CORES):
            pairs.append((i * CORES + c, (i + 1) * CORES + c))
            pairs.append(((planes - 1 - i) * CORES + c, (planes - 2 - i) * CORES + c))
        return lax.ppermute(value, "batch", pairs)

    x = hidden_in.reshape(SEGS, heads, piece, width)
    quarter = lambda m: lax.dynamic_index_in_dim(x, h ^ m, axis=1, keepdims=False)
    blocks = [quarter(0)] + [over_head(quarter(m), m) for m in range(1, heads)]
    weights = [w_query, w_key, w_value, w_beta]
    partner = [over_core(w) for w in weights]
    pos = [mem_pos[0]] + [over_z(mem_pos[0], j) for j in range(1, planes)]
    normed = call(
        functools.partial(norm_kernel, heads, full_width),
        [ids] + blocks,
        [shape((piece, width), bf16)] * (SEGS * planes),
        [pltpu.VMEM((heads, SEGS, piece, width), bf16)],
        name="norm",
    )
    y = [w_out, over_z(w_out, 1)]
    parts = []
    for s in range(SEGS):
        mine = normed[s * planes : (s + 1) * planes]
        held = [mine[0]] + [over_z(mine[j], j) for j in range(1, planes)]
        held = jnp.stack(held)
        pieces = [held] + [over_head(held, m) for m in range(1, heads)]
        parts.append(
            call(
                functools.partial(project_kernel, heads, s, mem_rows, min(256, features)),
                [ids] + pieces + pos + weights + partner,
                [shape((seg_rows + 2 * mem_rows + local_heads, features), bf16)] * planes,
                [
                    pltpu.VMEM((planes, seg_rows, width), bf16),
                    pltpu.VMEM((planes, mem_rows, width), bf16),
                ],
                flops=2 * planes * width * features * (seg_rows + 2 * mem_rows),
                name="project",
            )
        )
    r11, r10 = edge(w_out, 1), edge(y[1], 1)
    r21, r20 = edge(r11, 2), edge(r10, 2)
    outer = (z == 0) | (z == planes - 1)
    y = y + [jnp.where(outer, r21, r10), jnp.where(outer, r20, r11)]
    y_partner = [over_core(v) for v in y]
    add = lambda a, c: (a.astype(f32) + c.astype(f32)).astype(bf16)
    state = memory_in[0]
    outs = []
    for s in range(SEGS):
        u = parts[s]
        t03 = edge(u[3], 0)
        t02 = edge(u[2], 0)
        t01 = edge(u[1], 0)
        t13 = edge(add(u[2], t03), 1)
        t12 = edge(add(u[3], t02), 1)
        t23 = edge(add(u[1], t13), 2)
        readout, state = call(
            functools.partial(recur_kernel, 4, seg_rows, mem_rows, local_heads),
            [ids, u[0], t01, t12, t23, state],
            [shape((seg_rows, features), bf16), shape(state.shape, f32)],
            name="recur",
        )
        mixed = call(
            functools.partial(out_kernel, heads),
            [ids, readout] + y + y_partner,
            [shape((seg_rows, width), f32)] + [shape((seg_rows, width), bf16)] * (heads - 1),
            [pltpu.VMEM((heads, seg_rows, width), f32)],
            flops=2 * seg_rows * features * full_width,
            name="out",
        )
        total = mixed[0]
        for m in range(1, heads):
            total = total + over_head(mixed[m], m).astype(f32)
        rows = hidden_in[0, s * seg_rows : (s + 1) * seg_rows].astype(f32)
        outs.append((total + rows).astype(bf16))
    return (jnp.concatenate(outs, axis=0)[None], state[None])


def solution(mesh):
    heads, batch = mesh.shape["head"], mesh.shape["batch"]
    planes = batch // CORES

    def body(*arrays):
        return line_body(planes, heads, *arrays) if planes == heads == 4 else general_body(*arrays)

    in_specs = (
        P("batch", None, "head"),
        P("batch", "head"),
        P("batch", "head"),
        P("batch", "head"),
        P("batch", "head"),
        P("head", "batch"),
        P("batch", None, None),
        P("batch", "head", None, None),
    )
    out_specs = (P("batch", None, "head"), P("batch", "head", None, None))
    return jax.shard_map(body, mesh=mesh, in_specs=in_specs, out_specs=out_specs, check_vma=False)
```

```python
import functools

import jax
import jax.numpy as jnp
from jax import lax
from jax.experimental import pallas as pl
from jax.experimental.pallas import tpu as pltpu
from jax.sharding import PartitionSpec as P

SEGS = 2
CORES = 2
PAD = 8
epsilon = 1e-05


def recur(query, keys, values, beta, state):
    highest = lax.Precision.HIGHEST
    readouts = []
    for segment in range(query.shape[1]):
        readouts.append(
            jnp.einsum("bhij,blhj->blhi", state, query[:, segment], precision=highest).astype(
                jnp.bfloat16
            )
        )
        recalled = jnp.einsum("bhij,bmhj->bmhi", state, keys[:, segment], precision=highest)
        change = beta[:, segment][..., None] * (values[:, segment] - recalled)
        state = state + jnp.einsum("bmhi,bmhj->bhij", change, keys[:, segment], precision=highest)
    return (jnp.stack(readouts, axis=1), state)


def general_body(hidden_in, w_query, w_key, w_value, w_beta, w_out, mem_pos, memory_in):
    seq_count, row_count, local_width = hidden_in.shape
    seg_rows = row_count // SEGS
    mem_count = mem_pos.shape[2]
    local_heads = w_beta.shape[1]
    local_features = w_query.shape[1]
    head_size = local_features // local_heads
    x_float = hidden_in.astype(jnp.float32)
    whole = lax.all_gather(hidden_in, "head", axis=2, tiled=True)
    whole_float = whole.astype(jnp.float32)
    mean_square = jnp.mean(whole_float * whole_float, axis=2, keepdims=True)
    normed = (whole_float * lax.rsqrt(mean_square + epsilon)).astype(jnp.bfloat16)
    full_width = normed.shape[2]
    offsets = (jnp.arange(SEGS, dtype=jnp.int32) * seg_rows)[None, :, None]
    picked = (mem_pos + offsets).reshape(seq_count, SEGS * mem_count)
    memory_rows = jax.vmap(lambda block, where: jnp.take(block, where, axis=0))(normed, picked)
    memory_rows = memory_rows.reshape(seq_count * SEGS * mem_count, full_width)
    token_rows = normed.reshape(seq_count * row_count, full_width)
    piece_query = lax.all_gather(w_query, "batch", axis=0, tiled=True)
    piece_key = lax.all_gather(w_key, "batch", axis=0, tiled=True)
    piece_value = lax.all_gather(w_value, "batch", axis=0, tiled=True)
    piece_beta = lax.all_gather(w_beta, "batch", axis=0, tiled=True)
    query = jnp.dot(token_rows, piece_query, preferred_element_type=jnp.float32)
    keys = jnp.dot(memory_rows, piece_key, preferred_element_type=jnp.float32)
    values = jnp.dot(memory_rows, piece_value, preferred_element_type=jnp.float32)
    logits = jnp.dot(memory_rows, piece_beta, preferred_element_type=jnp.float32)
    query = (query * head_size ** (-0.5)).reshape(seq_count, SEGS, seg_rows, local_heads, head_size)
    keys = keys.reshape(seq_count, SEGS, mem_count, local_heads, head_size)
    keys = keys * lax.rsqrt(jnp.sum(keys * keys, axis=-1, keepdims=True) + 1e-06)
    values = values.reshape(seq_count, SEGS, mem_count, local_heads, head_size)
    beta = jax.nn.sigmoid(logits).reshape(seq_count, SEGS, mem_count, local_heads)
    readout, state = recur(query, keys, values, beta, memory_in)
    readout = readout.reshape(seq_count * row_count, local_features)
    terms = jnp.dot(
        readout,
        lax.all_gather(w_out, "batch", axis=1, tiled=True),
        preferred_element_type=jnp.float32,
    )
    mixed = lax.psum_scatter(terms, "head", scatter_dimension=1, tiled=True)
    hidden_out = (mixed + x_float.reshape(seq_count * row_count, local_width)).astype(jnp.bfloat16)
    return (hidden_out.reshape(hidden_in.shape), state)


VM = pl.BlockSpec(memory_space=pltpu.VMEM)
SM = pl.BlockSpec(memory_space=pltpu.SMEM)


def call(kernel, args, outs, scratch=(), flops=0, grid=(), specs=None, out_specs=None):
    size = sum(a.size * a.dtype.itemsize for a in list(args[1:]) + list(outs))
    return pl.pallas_call(
        kernel,
        out_shape=outs,
        grid=grid,
        in_specs=[SM] + list(specs or [VM] * (len(args) - 1)),
        out_specs=list(out_specs or [VM] * len(outs)),
        scratch_shapes=list(scratch),
        cost_estimate=pl.CostEstimate(flops=flops, bytes_accessed=size, transcendentals=0),
    )(*args)


def whole(value):
    return pl.BlockSpec(value.shape, lambda n: (0,) * len(value.shape))


def columns_of(value, tile):
    return pl.BlockSpec((value.shape[0], tile), lambda n: (0, n))


def norm_kernel(heads, width, ids, *refs):
    blocks = refs[:heads]
    outs = refs[heads:-1]
    held = refs[-1]
    square = None
    for block in blocks:
        value = block[...].astype(jnp.float32)
        part = jnp.sum(value * value, axis=-1, keepdims=True)
        square = part if square is None else square + part
    scale = lax.rsqrt(square / width + epsilon)
    for m, block in enumerate(blocks):
        held[m] = (block[...].astype(jnp.float32) * scale).astype(jnp.bfloat16)
    mix = ids[0] ^ ids[1]
    for s in range(SEGS):
        for j in range(heads):
            outs[s * heads + j][...] = held[mix ^ j, s]


def project_kernel(heads, seg, size, groups, ids, *refs):
    pieces = refs[:heads]
    pos = refs[heads : 2 * heads]
    own = refs[2 * heads : 2 * heads + 4]
    other = refs[2 * heads + 4 : 2 * heads + 8]
    outs = refs[2 * heads + 8 : -3]
    rows, picked, logits = refs[-3:]
    piece = pieces[0].shape[1]
    seg_rows = piece * heads
    mem_rows = pos[0].shape[1]
    depth = own[0].shape[0]
    mine = pl.ds(pl.multiple_of(ids[2] * depth, depth), depth)
    theirs = pl.ds(pl.multiple_of((1 - ids[2]) * depth, depth), depth)
    n = pl.program_id(0)

    @pl.when(n == 0)
    def _():
        for m in range(heads):
            start = pl.multiple_of((ids[0] ^ m) * piece, piece)
            for j in range(heads):
                rows[j, pl.ds(start, piece), :] = pieces[m][j]
        token = lax.broadcasted_iota(jnp.int32, (seg_rows, mem_rows), 0)
        contract = (((0,), (1,)), ((), ()))
        for j in range(heads):
            hot = jnp.where(token == pos[j][seg : seg + 1, :], 1.0, 0.0).astype(jnp.bfloat16)
            picked[j] = lax.dot_general(
                hot, rows[j], (((0,), (0,)), ((), ())), preferred_element_type=jnp.float32
            ).astype(jnp.bfloat16)
            logits[j] = lax.dot_general(
                own[3][...], picked[j, :, mine], contract, preferred_element_type=jnp.float32
            ) + lax.dot_general(
                other[3][...], picked[j, :, theirs], contract, preferred_element_type=jnp.float32
            )

    flat = lambda ref, part: ref[:, :, part].reshape(-1, depth)

    def product(source, weight):
        return jnp.dot(
            flat(source, mine), own[weight][...], preferred_element_type=jnp.float32
        ) + jnp.dot(
            flat(source, theirs), other[weight][...], preferred_element_type=jnp.float32
        )

    results = (
        (product(rows, 0).astype(jnp.bfloat16), seg_rows),
        (product(picked, 1).astype(jnp.bfloat16), mem_rows),
        (product(picked, 2).astype(jnp.bfloat16), mem_rows),
    )
    tile = own[0].shape[1]
    for g, group in enumerate(groups):
        for j in range(heads):
            out = outs[g * heads + j]
            top = 0
            for kind in group:
                result, count = results[kind]
                out[top : top + count, :] = result[j * count : (j + 1) * count]
                top += count
            if 2 in group:
                for k in range(tile // size):
                    logit = logits[j, pl.ds(n * (tile // size) + k, 1), :]
                    shown = jnp.broadcast_to(logit, (out.shape[0] - top, mem_rows))
                    shown = jnp.concatenate([shown, jnp.zeros_like(shown)], axis=1)
                    out[top:, k * size : (k + 1) * size] = shown[:, :size].astype(jnp.bfloat16)


HIGHEST = lax.Precision.HIGHEST
ACROSS = (((1,), (1,)), ((), ()))


def summed(parts, held):
    value = parts[0][...].astype(jnp.float32)
    for part in parts[1:]:
        value = value + part[...].astype(jnp.float32)
    held[...] = value


def read_states(held, states, readout, seg_rows):
    size = readout.shape[1] // len(states)
    for head, state in enumerate(states):
        columns = slice(head * size, (head + 1) * size)
        query = held[:seg_rows, columns] * size ** (-0.5)
        readout[:, columns] = lax.dot_general(
            query, state, ACROSS, precision=HIGHEST, preferred_element_type=jnp.float32
        ).astype(jnp.bfloat16)


def update_states(held, states, state_out, first, mem_rows):
    size = states[0].shape[-1]
    kept = []
    for head, state in enumerate(states):
        columns = slice(head * size, (head + 1) * size)
        keys = held[first : first + mem_rows, columns]
        keys = keys * lax.rsqrt(jnp.sum(keys * keys, axis=-1, keepdims=True) + 1e-06)
        recalled = lax.dot_general(
            keys, state, ACROSS, precision=HIGHEST, preferred_element_type=jnp.float32
        )
        kept.append((keys, recalled))
    changes = []
    for head, (keys, recalled) in enumerate(kept):
        columns = slice(head * size, (head + 1) * size)
        values = held[first + mem_rows : first + 2 * mem_rows, columns]
        logits = held[first + 2 * mem_rows :, columns]
        beta = jax.nn.sigmoid(logits).T[:mem_rows, :1]
        changes.append(beta * (values - recalled))
    for head, state in enumerate(states):
        state_out[head] = state + lax.dot_general(
            changes[head],
            kept[head][0],
            (((0,), (0,)), ((), ())),
            precision=HIGHEST,
            preferred_element_type=jnp.float32,
        )


def heads_in(state_in):
    return [state_in[head] for head in range(state_in.shape[0])]


def both_kernel(count, seg_rows, mem_rows, ids, *refs):
    state_in, readout, state_out, held = refs[count:]
    summed(refs[:count], held)
    states = heads_in(state_in)
    read_states(held, states, readout, seg_rows)
    update_states(held, states, state_out, seg_rows, mem_rows)


def read_kernel(count, seg_rows, ids, *refs):
    state_in, readout, held = refs[count:]
    summed(refs[:count], held)
    read_states(held, heads_in(state_in), readout, seg_rows)


def update_kernel(count, mem_rows, ids, *refs):
    state_in, state_out, held = refs[count:]
    summed(refs[:count], held)
    update_states(held, heads_in(state_in), state_out, 0, mem_rows)


def out_kernel(heads, ids, *refs):
    readout = refs[0]
    own = refs[1 : 1 + heads]
    other = refs[1 + heads : 1 + 2 * heads]
    outs = refs[1 + 2 * heads : 1 + 3 * heads]
    held = refs[-1]
    tile = own[0].shape[1]
    n = pl.program_id(0)
    steps = pl.num_programs(0)
    mix = ids[0] ^ ids[1]
    rows = readout[...]
    for j in range(heads):
        for core, weights in ((ids[2], own[j]), (1 - ids[2], other[j])):
            start = pl.multiple_of((core * steps + n) * tile, tile)
            held[mix ^ j, :, pl.ds(start, tile)] = jnp.dot(
                rows, weights[...], preferred_element_type=jnp.float32
            )

    @pl.when(n == steps - 1)
    def _():
        for m in range(heads):
            outs[m][...] = held[m].astype(outs[m].dtype)


def line_body(planes, heads, *arrays):
    hidden_in, w_query, w_key, w_value, w_beta, w_out, mem_pos, memory_in = arrays
    row_count, width = hidden_in.shape[1:]
    seg_rows, mem_rows = row_count // SEGS, mem_pos.shape[2]
    piece = seg_rows // heads
    local_heads = w_beta.shape[1]
    features = w_query.shape[1]
    full_width = width * heads
    size = features // local_heads
    tile = min(256, features)
    bf16, f32 = jnp.bfloat16, jnp.float32
    h, b = lax.axis_index("head"), lax.axis_index("batch")
    z, core = b // CORES, b % CORES
    ids = jnp.stack([h, z, core]).astype(jnp.int32)
    shape = jax.ShapeDtypeStruct

    def over_head(value, m):
        return lax.ppermute(value, "head", [(i, i ^ m) for i in range(heads)])

    def over_z(value, j):
        pairs = [(i, i ^ (j * CORES)) for i in range(planes * CORES)]
        return lax.ppermute(value, "batch", pairs)

    def over_core(value):
        return lax.ppermute(value, "batch", [(i, i ^ 1) for i in range(planes * CORES)])

    def edge(value, i):
        pairs = []
        for c in range(CORES):
            pairs.append((i * CORES + c, (i + 1) * CORES + c))
            pairs.append(((planes - 1 - i) * CORES + c, (planes - 2 - i) * CORES + c))
        return lax.ppermute(value, "batch", pairs)

    x = hidden_in.reshape(SEGS, heads, piece, width)
    quarter = lambda m: lax.dynamic_index_in_dim(x, h ^ m, axis=1, keepdims=False)
    blocks = [quarter(0)] + [over_head(quarter(m), m) for m in range(1, heads)]
    weights = [w_query, w_key, w_value, w_beta]
    partner = [over_core(w) for w in weights]
    pos = [mem_pos[0]] + [over_z(mem_pos[0], j) for j in range(1, planes)]
    normed = call(
        functools.partial(norm_kernel, heads, full_width),
        [ids] + blocks,
        [shape((piece, width), bf16)] * (SEGS * planes),
        [pltpu.VMEM((heads, SEGS, piece, width), bf16)],
    )
    y = [w_out, over_z(w_out, 1)]
    parts = []
    last = SEGS - 1
    groups = [((0, 1, 2),)] * last + [((0,), (1, 2))]
    for s in range(SEGS):
        kinds = (seg_rows, mem_rows, mem_rows + PAD)
        counts = [sum(kinds[kind] for kind in group) for group in groups[s]]
        mine = normed[s * planes : (s + 1) * planes]
        held = [mine[0]] + [over_z(mine[j], j) for j in range(1, planes)]
        held = jnp.stack(held)
        pieces = [held] + [over_head(held, m) for m in range(1, heads)]
        parts.append(
            call(
                functools.partial(project_kernel, heads, s, size, groups[s]),
                [ids] + pieces + pos + weights + partner,
                [shape((count, features), bf16) for count in counts for _ in range(planes)],
                [
                    pltpu.VMEM((planes, seg_rows, width), bf16),
                    pltpu.VMEM((planes, mem_rows, width), bf16),
                    pltpu.VMEM((planes, local_heads, mem_rows), f32),
                ],
                flops=2 * planes * width * features * (seg_rows + 2 * mem_rows),
                grid=(features // tile,),
                specs=[whole(v) for v in pieces + pos]
                + [columns_of(v, tile) for v in weights[:3]]
                + [whole(w_beta)]
                + [columns_of(v, tile) for v in weights[:3]]
                + [whole(w_beta)],
                out_specs=[
                    pl.BlockSpec((count, tile), lambda n: (0, n))
                    for count in counts
                    for _ in range(planes)
                ],
            )
        )
    r11, r10 = edge(w_out, 1), edge(y[1], 1)
    r21, r20 = edge(r11, 2), edge(r10, 2)
    outer = (z == 0) | (z == planes - 1)
    y = y + [jnp.where(outer, r21, r10), jnp.where(outer, r20, r11)]
    y_partner = [over_core(v) for v in y]
    add = lambda a, c: (a.astype(f32) + c.astype(f32)).astype(bf16)

    def line_sum(u):
        t03 = edge(u[3], 0)
        t02 = edge(u[2], 0)
        t01 = edge(u[1], 0)
        t13 = edge(add(u[2], t03), 1)
        t12 = edge(add(u[3], t02), 1)
        t23 = edge(add(u[1], t13), 2)
        return [u[0], t01, t12, t23]

    read_shape = shape((seg_rows, features), bf16)
    state_shape = shape(memory_in.shape[1:], f32)

    def emit(readout, s):
        mixed = call(
            functools.partial(out_kernel, heads),
            [ids, readout] + y + y_partner,
            [shape((seg_rows, width), f32)] + [shape((seg_rows, width), bf16)] * (heads - 1),
            [pltpu.VMEM((heads, seg_rows, width), f32)],
            flops=2 * seg_rows * features * full_width,
            grid=(w_out.shape[1] // tile,),
            specs=[whole(readout)] + [columns_of(v, tile) for v in y + y_partner],
            out_specs=[pl.BlockSpec((seg_rows, width), lambda n: (0, 0))] * heads,
        )
        total = mixed[0]
        for m in range(1, heads):
            total = total + over_head(mixed[m], m).astype(f32)
        rows = hidden_in[0, s * seg_rows : (s + 1) * seg_rows].astype(f32)
        return (total + rows).astype(bf16)

    state = memory_in[0]
    outs = []
    for s in range(last):
        sums = line_sum(parts[s])
        readout, state = call(
            functools.partial(both_kernel, 4, seg_rows, mem_rows),
            [ids] + sums + [state],
            [read_shape, state_shape],
            scratch=[pltpu.VMEM(sums[0].shape, f32)],
        )
        outs.append(emit(readout, s))
    sums = line_sum(parts[last][:planes])
    readout = call(
        functools.partial(read_kernel, 4, seg_rows),
        [ids] + sums + [state],
        [read_shape],
        scratch=[pltpu.VMEM(sums[0].shape, f32)],
    )[0]
    outs.append(emit(readout, last))
    sums = line_sum(parts[last][planes:])
    state = call(
        functools.partial(update_kernel, 4, mem_rows),
        [ids] + sums + [state],
        [state_shape],
        scratch=[pltpu.VMEM(sums[0].shape, f32)],
    )[0]
    return (jnp.concatenate(outs, axis=0)[None], state[None])


def solution(mesh):
    heads, batch = mesh.shape["head"], mesh.shape["batch"]
    planes = batch // CORES
    lined = planes == heads == 4

    def body(*arrays):
        if not lined:
            return general_body(*arrays)
        return line_body(planes, heads, *arrays)

    in_specs = (
        P("batch", None, "head"),
        P("batch", "head"),
        P("batch", "head"),
        P("batch", "head"),
        P("batch", "head"),
        P("head", "batch"),
        P("batch", None, None),
        P("batch", "head", None, None),
    )
    out_specs = (P("batch", None, "head"), P("batch", "head", None, None))
    return jax.shard_map(body, mesh=mesh, in_specs=in_specs, out_specs=out_specs, check_vma=False)
```

```python
import functools

import jax
import jax.numpy as jnp
from jax import lax
from jax.experimental import pallas as pl
from jax.experimental.pallas import tpu as pltpu
from jax.sharding import PartitionSpec as P

SEGS = 2
CORES = 2
PAD = 8
epsilon = 1e-05


def recur(query, keys, values, beta, state):
    highest = lax.Precision.HIGHEST
    readouts = []
    for segment in range(query.shape[1]):
        readouts.append(
            jnp.einsum("bhij,blhj->blhi", state, query[:, segment], precision=highest).astype(
                jnp.bfloat16
            )
        )
        recalled = jnp.einsum("bhij,bmhj->bmhi", state, keys[:, segment], precision=highest)
        change = beta[:, segment][..., None] * (values[:, segment] - recalled)
        state = state + jnp.einsum("bmhi,bmhj->bhij", change, keys[:, segment], precision=highest)
    return (jnp.stack(readouts, axis=1), state)


def general_body(hidden_in, w_query, w_key, w_value, w_beta, w_out, mem_pos, memory_in):
    seq_count, row_count, local_width = hidden_in.shape
    seg_rows = row_count // SEGS
    mem_count = mem_pos.shape[2]
    local_heads = w_beta.shape[1]
    local_features = w_query.shape[1]
    head_size = local_features // local_heads
    x_float = hidden_in.astype(jnp.float32)
    whole = lax.all_gather(hidden_in, "head", axis=2, tiled=True)
    whole_float = whole.astype(jnp.float32)
    mean_square = jnp.mean(whole_float * whole_float, axis=2, keepdims=True)
    normed = (whole_float * lax.rsqrt(mean_square + epsilon)).astype(jnp.bfloat16)
    full_width = normed.shape[2]
    offsets = (jnp.arange(SEGS, dtype=jnp.int32) * seg_rows)[None, :, None]
    picked = (mem_pos + offsets).reshape(seq_count, SEGS * mem_count)
    memory_rows = jax.vmap(lambda block, where: jnp.take(block, where, axis=0))(normed, picked)
    memory_rows = memory_rows.reshape(seq_count * SEGS * mem_count, full_width)
    token_rows = normed.reshape(seq_count * row_count, full_width)
    piece_query = lax.all_gather(w_query, "batch", axis=0, tiled=True)
    piece_key = lax.all_gather(w_key, "batch", axis=0, tiled=True)
    piece_value = lax.all_gather(w_value, "batch", axis=0, tiled=True)
    piece_beta = lax.all_gather(w_beta, "batch", axis=0, tiled=True)
    query = jnp.dot(token_rows, piece_query, preferred_element_type=jnp.float32)
    keys = jnp.dot(memory_rows, piece_key, preferred_element_type=jnp.float32)
    values = jnp.dot(memory_rows, piece_value, preferred_element_type=jnp.float32)
    logits = jnp.dot(memory_rows, piece_beta, preferred_element_type=jnp.float32)
    query = (query * head_size ** (-0.5)).reshape(seq_count, SEGS, seg_rows, local_heads, head_size)
    keys = keys.reshape(seq_count, SEGS, mem_count, local_heads, head_size)
    keys = keys * lax.rsqrt(jnp.sum(keys * keys, axis=-1, keepdims=True) + 1e-06)
    values = values.reshape(seq_count, SEGS, mem_count, local_heads, head_size)
    beta = jax.nn.sigmoid(logits).reshape(seq_count, SEGS, mem_count, local_heads)
    readout, state = recur(query, keys, values, beta, memory_in)
    readout = readout.reshape(seq_count * row_count, local_features)
    terms = jnp.dot(
        readout,
        lax.all_gather(w_out, "batch", axis=1, tiled=True),
        preferred_element_type=jnp.float32,
    )
    mixed = lax.psum_scatter(terms, "head", scatter_dimension=1, tiled=True)
    hidden_out = (mixed + x_float.reshape(seq_count * row_count, local_width)).astype(jnp.bfloat16)
    return (hidden_out.reshape(hidden_in.shape), state)


VM = pl.BlockSpec(memory_space=pltpu.VMEM)
SM = pl.BlockSpec(memory_space=pltpu.SMEM)


def call(kernel, args, outs, scratch=(), flops=0, grid=(), specs=None, out_specs=None, room=24):
    size = sum(a.size * a.dtype.itemsize for a in list(args[1:]) + list(outs))
    return pl.pallas_call(
        kernel,
        out_shape=outs,
        grid=grid,
        in_specs=[SM] + list(specs or [VM] * (len(args) - 1)),
        out_specs=list(out_specs or [VM] * len(outs)),
        scratch_shapes=list(scratch),
        compiler_params=pltpu.CompilerParams(vmem_limit_bytes=room << 20),
        cost_estimate=pl.CostEstimate(flops=flops, bytes_accessed=size, transcendentals=0),
    )(*args)


def whole(value):
    return pl.BlockSpec(value.shape, lambda n: (0,) * len(value.shape))


def columns_of(value, tile):
    return pl.BlockSpec((value.shape[0], tile), lambda n: (0, n))


def norm_kernel(heads, width, ids, *refs):
    blocks = refs[:heads]
    places = refs[heads]
    outs = refs[heads + 1 : -1]
    held = refs[-1]
    square = None
    for block in blocks:
        value = block[...].astype(jnp.float32)
        part = jnp.sum(value * value, axis=-1, keepdims=True)
        square = part if square is None else square + part
    scale = lax.rsqrt(square / width + epsilon)
    for m, block in enumerate(blocks):
        held[m] = (block[...].astype(jnp.float32) * scale).astype(jnp.bfloat16)
    mix = ids[0] ^ ids[1]
    rows, mem = held.shape[2], places.shape[1]
    for s in range(SEGS):
        for j in range(heads):
            out = outs[s * heads + j]
            out[:rows, :] = held[mix ^ j, s]
            if s == 0:
                out[rows:, :] = jnp.zeros((PAD, out.shape[1]), jnp.bfloat16)
                shown = places[...].astype(jnp.float32).astype(jnp.bfloat16)
                out[rows : rows + SEGS, :mem] = shown


def gather_pieces(heads, ids, pieces, rows):
    piece = pieces[0].shape[1]
    for m in range(heads):
        start = pl.multiple_of((ids[0] ^ m) * piece, piece)
        for j in range(heads):
            rows[j, pl.ds(start, piece), :] = pieces[m][j]


def weight_rows(ids, depth):
    mine = pl.ds(pl.multiple_of(ids[2] * depth, depth), depth)
    theirs = pl.ds(pl.multiple_of((1 - ids[2]) * depth, depth), depth)
    return mine, theirs


def product(source, parts, own, other):
    depth = own.shape[0]
    mine, theirs = parts
    return (
        jnp.dot(
            source[:, :, mine].reshape(-1, depth), own[...], preferred_element_type=jnp.float32
        )
        + jnp.dot(
            source[:, :, theirs].reshape(-1, depth), other[...], preferred_element_type=jnp.float32
        )
    ).astype(jnp.bfloat16)


def query_kernel(heads, ids, *refs):
    pieces = refs[:heads]
    own, other = refs[heads : heads + 2]
    outs = refs[heads + 2 : -1]
    rows = refs[-1]

    @pl.when(pl.program_id(0) == 0)
    def _():
        gather_pieces(heads, ids, pieces, rows)

    result = product(rows, weight_rows(ids, own.shape[0]), own, other)
    count = rows.shape[1]
    for j in range(heads):
        outs[j][...] = result[j * count : (j + 1) * count]


def project_kernel(heads, mem, size, ids, *refs):
    pieces = [refs[:heads], refs[heads : 2 * heads]]
    pos = refs[2 * heads : 3 * heads]
    own = refs[3 * heads : 3 * heads + 4]
    other = refs[3 * heads + 4 : 3 * heads + 8]
    outs = refs[3 * heads + 8 : -4]
    first, rows, picked, logits = refs[-4:]
    seg_rows = rows.shape[1]
    piece = pieces[0][0].shape[1]
    parts = weight_rows(ids, own[0].shape[0])
    n = pl.program_id(0)

    @pl.when(n == 0)
    def _():
        token = lax.broadcasted_iota(jnp.int32, (seg_rows, mem), 0).astype(jnp.float32)
        contract = (((0,), (1,)), ((), ()))
        for s, source in enumerate((first, rows)):
            gather_pieces(heads, ids, pieces[s], source)
            for j in range(heads):
                where = pos[j][piece:, :][s : s + 1, :mem].astype(jnp.float32)
                hot = jnp.where(token == where, 1.0, 0.0).astype(jnp.bfloat16)
                chosen = lax.dot_general(
                    hot, source[j], (((0,), (0,)), ((), ())), preferred_element_type=jnp.float32
                ).astype(jnp.bfloat16)
                picked[s * heads + j] = chosen
                logits[s * heads + j] = sum(
                    lax.dot_general(
                        weight[...],
                        picked[s * heads + j, :, part],
                        contract,
                        preferred_element_type=jnp.float32,
                    )
                    for weight, part in ((own[3], parts[0]), (other[3], parts[1]))
                )

    query = product(rows, parts, own[0], other[0])
    pairs = [product(picked, parts, own[kind], other[kind]) for kind in (1, 2)]
    tile = own[0].shape[1]
    for j in range(heads):
        outs[j][:seg_rows, :] = query[j * seg_rows : (j + 1) * seg_rows]
    for index in range(SEGS * heads):
        out = outs[index]
        top = seg_rows if index < heads else 0
        for result in pairs:
            out[top : top + mem, :] = result[index * mem : (index + 1) * mem]
            top += mem
        for k in range(tile // size):
            logit = logits[index, pl.ds(n * (tile // size) + k, 1), :]
            shown = jnp.broadcast_to(logit, (PAD, mem)).astype(jnp.bfloat16)
            out[top:, k * size : k * size + mem] = shown
            out[top:, k * size + mem : (k + 1) * size] = jnp.zeros(
                (PAD, size - mem), jnp.bfloat16
            )


HIGHEST = lax.Precision.HIGHEST
ACROSS = (((1,), (1,)), ((), ()))


def summed(parts, held):
    value = parts[0][...].astype(jnp.float32)
    for part in parts[1:]:
        value = value + part[...].astype(jnp.float32)
    held[...] = value


def read_states(held, states, readout, seg_rows):
    size = readout.shape[1] // len(states)
    for head, state in enumerate(states):
        columns = slice(head * size, (head + 1) * size)
        query = held[:seg_rows, columns] * size ** (-0.5)
        readout[:, columns] = lax.dot_general(
            query, state, ACROSS, precision=HIGHEST, preferred_element_type=jnp.float32
        ).astype(jnp.bfloat16)


def update_states(held, states, state_out, first, mem_rows):
    size = states[0].shape[-1]
    kept = []
    for head, state in enumerate(states):
        columns = slice(head * size, (head + 1) * size)
        keys = held[first : first + mem_rows, columns]
        keys = keys * lax.rsqrt(jnp.sum(keys * keys, axis=-1, keepdims=True) + 1e-06)
        recalled = lax.dot_general(
            keys, state, ACROSS, precision=HIGHEST, preferred_element_type=jnp.float32
        )
        kept.append((keys, recalled))
    changes = []
    for head, (keys, recalled) in enumerate(kept):
        columns = slice(head * size, (head + 1) * size)
        values = held[first + mem_rows : first + 2 * mem_rows, columns]
        logits = held[first + 2 * mem_rows :, columns]
        beta = jax.nn.sigmoid(logits).T[:mem_rows, :1]
        changes.append(beta * (values - recalled))
    later = []
    for head, state in enumerate(states):
        later.append(
            state
            + lax.dot_general(
                changes[head],
                kept[head][0],
                (((0,), (0,)), ((), ())),
                precision=HIGHEST,
                preferred_element_type=jnp.float32,
            )
        )
        state_out[head] = later[head]
    return later


def heads_in(state_in):
    return [state_in[head] for head in range(state_in.shape[0])]


def both_kernel(count, seg_rows, mem_rows, ids, *refs):
    state_in, readout, state_out, held = refs[count:]
    summed(refs[:count], held)
    states = update_states(held, heads_in(state_in), state_out, seg_rows, mem_rows)
    read_states(held, states, readout, seg_rows)


def read_kernel(count, seg_rows, ids, *refs):
    state_in, readout, held = refs[count:]
    summed(refs[:count], held)
    read_states(held, heads_in(state_in), readout, seg_rows)


def update_kernel(count, mem_rows, ids, *refs):
    state_in, state_out, held = refs[count:]
    summed(refs[:count], held)
    update_states(held, heads_in(state_in), state_out, 0, mem_rows)


def out_kernel(heads, ids, *refs):
    readout = refs[0]
    own = refs[1 : 1 + heads]
    other = refs[1 + heads : 1 + 2 * heads]
    outs = refs[1 + 2 * heads : 1 + 3 * heads]
    held = refs[-1]
    tile = own[0].shape[1]
    n = pl.program_id(0)
    steps = pl.num_programs(0)
    mix = ids[0] ^ ids[1]
    rows = readout[...]
    for j in range(heads):
        for core, weights in ((ids[2], own[j]), (1 - ids[2], other[j])):
            start = pl.multiple_of((core * steps + n) * tile, tile)
            held[mix ^ j, :, pl.ds(start, tile)] = jnp.dot(
                rows, weights[...], preferred_element_type=jnp.float32
            )

    @pl.when(n == steps - 1)
    def _():
        for m in range(heads):
            outs[m][...] = held[m].astype(outs[m].dtype)


def line_body(planes, heads, *arrays):
    hidden_in, w_query, w_key, w_value, w_beta, w_out, mem_pos, memory_in = arrays
    row_count, width = hidden_in.shape[1:]
    seg_rows, mem_rows = row_count // SEGS, mem_pos.shape[2]
    piece = seg_rows // heads
    local_heads = w_beta.shape[1]
    features = w_query.shape[1]
    full_width = width * heads
    size = features // local_heads
    tile = min(256, features)
    bf16, f32 = jnp.bfloat16, jnp.float32
    h, b = lax.axis_index("head"), lax.axis_index("batch")
    z, core = b // CORES, b % CORES
    ids = jnp.stack([h, z, core]).astype(jnp.int32)
    shape = jax.ShapeDtypeStruct

    def over_head(value, m):
        return lax.ppermute(value, "head", [(i, i ^ m) for i in range(heads)])

    def over_z(value, j):
        pairs = [(i, i ^ (j * CORES)) for i in range(planes * CORES)]
        return lax.ppermute(value, "batch", pairs)

    def over_core(value):
        return lax.ppermute(value, "batch", [(i, i ^ 1) for i in range(planes * CORES)])

    def edge(value, i):
        pairs = []
        for c in range(CORES):
            pairs.append((i * CORES + c, (i + 1) * CORES + c))
            pairs.append(((planes - 1 - i) * CORES + c, (planes - 2 - i) * CORES + c))
        return lax.ppermute(value, "batch", pairs)

    halves = jnp.split(w_out, 2, axis=0)
    near = [over_z(half, 1) for half in halves]
    across = [edge(half, 1) for half in halves]
    x = hidden_in.reshape(SEGS, heads, piece, width)
    quarter = lambda m: lax.dynamic_index_in_dim(x, h ^ m, axis=1, keepdims=False)
    blocks = [quarter(0)] + [over_head(quarter(m), m) for m in range(1, heads)]
    weights = [w_query, w_key, w_value, w_beta]
    partner = [over_core(w) for w in weights]
    normed = call(
        functools.partial(norm_kernel, heads, full_width),
        [ids] + blocks + [mem_pos[0]],
        [shape((piece + PAD, width), bf16)] * planes + [shape((piece, width), bf16)] * planes,
        [pltpu.VMEM((heads, SEGS, piece, width), bf16)],
        room=8,
    )
    pieces = []
    for s in range(SEGS):
        mine = normed[s * planes : (s + 1) * planes]
        got = [mine[0]] + [over_z(mine[j], j) for j in range(1, planes)]
        if s == 0:
            pos = got
        held = jnp.stack([value[:piece] for value in got])
        pieces.append([held] + [over_head(held, m) for m in range(1, heads)])
    tiles = lambda values: [columns_of(v, tile) for v in values]
    column_tile = lambda count: pl.BlockSpec((count, tile), lambda n: (0, n))
    queries = call(
        functools.partial(query_kernel, heads),
        [ids] + pieces[0] + [w_query, partner[0]],
        [shape((seg_rows, features), bf16)] * planes,
        [pltpu.VMEM((planes, seg_rows, width), bf16)],
        flops=2 * planes * width * features * seg_rows,
        room=16,
        grid=(features // tile,),
        specs=[whole(v) for v in pieces[0]] + tiles([w_query, partner[0]]),
        out_specs=[column_tile(seg_rows)] * planes,
    )
    few = 2 * mem_rows + PAD
    counts = [seg_rows + few] * planes + [few] * planes
    products = call(
        functools.partial(project_kernel, heads, mem_rows, size),
        [ids] + pieces[0] + pieces[1] + pos + weights + partner,
        [shape((count, features), bf16) for count in counts],
        [
            pltpu.VMEM((planes, seg_rows, width), bf16),
            pltpu.VMEM((planes, seg_rows, width), bf16),
            pltpu.VMEM((SEGS * planes, mem_rows, width), bf16),
            pltpu.VMEM((SEGS * planes, local_heads, mem_rows), f32),
        ],
        flops=2 * planes * width * features * (seg_rows + 4 * mem_rows),
        grid=(features // tile,),
        specs=[whole(v) for v in pieces[0] + pieces[1] + pos]
        + tiles(weights[:3])
        + [whole(w_beta)]
        + tiles(partner[:3])
        + [whole(w_beta)],
        out_specs=[column_tile(count) for count in counts],
    )
    y = [w_out, jnp.concatenate(near, axis=0)]
    r11, r10 = jnp.concatenate(across, axis=0), edge(y[1], 1)
    r21, r20 = edge(r11, 2), edge(r10, 2)
    outer = (z == 0) | (z == planes - 1)
    y = y + [jnp.where(outer, r21, r10), jnp.where(outer, r20, r11)]
    y_partner = [over_core(v) for v in y]
    add = lambda a, c: (a.astype(f32) + c.astype(f32)).astype(bf16)

    def line_sum(u):
        t03 = edge(u[3], 0)
        t02 = edge(u[2], 0)
        t13 = edge(add(u[2], t03), 1)
        t12 = edge(add(u[3], t02), 1)
        pair = over_z(add(u[1], t13), 1)
        return [u[0], pair, t12]

    read_shape = shape((seg_rows, features), bf16)
    state_shape = shape(memory_in.shape[1:], f32)

    def emit(readout, s):
        mixed = call(
            functools.partial(out_kernel, heads),
            [ids, readout] + y + y_partner,
            [shape((seg_rows, width), f32)] + [shape((seg_rows, width), bf16)] * (heads - 1),
            [pltpu.VMEM((heads, seg_rows, width), f32)],
            flops=2 * seg_rows * features * full_width,
            grid=(w_out.shape[1] // tile,),
            specs=[whole(readout)] + [columns_of(v, tile) for v in y + y_partner],
            out_specs=[pl.BlockSpec((seg_rows, width), lambda n: (0, 0))] * heads,
        )
        total = mixed[0]
        for m in range(1, heads):
            total = total + over_head(mixed[m], m).astype(f32)
        rows = hidden_in[0, s * seg_rows : (s + 1) * seg_rows].astype(f32)
        return (total + rows).astype(bf16)

    state = memory_in[0]
    sums = line_sum(queries)
    readout = call(
        functools.partial(read_kernel, 3, seg_rows),
        [ids] + sums + [state],
        [read_shape],
        room=8,
        scratch=[pltpu.VMEM(sums[0].shape, f32)],
    )[0]
    outs = [emit(readout, 0)]
    sums = line_sum(products[:planes])
    readout, state = call(
        functools.partial(both_kernel, 3, seg_rows, mem_rows),
        [ids] + sums + [state],
        [read_shape, state_shape],
        room=12,
        scratch=[pltpu.VMEM(sums[0].shape, f32)],
    )
    outs.append(emit(readout, 1))
    sums = line_sum(products[planes:])
    state = call(
        functools.partial(update_kernel, 3, mem_rows),
        [ids] + sums + [state],
        [state_shape],
        room=8,
        scratch=[pltpu.VMEM(sums[0].shape, f32)],
    )[0]
    return (jnp.concatenate(outs, axis=0)[None], state[None])


def solution(mesh):
    heads, batch = mesh.shape["head"], mesh.shape["batch"]
    planes = batch // CORES
    lined = planes == heads == 4

    def body(*arrays):
        if not lined:
            return general_body(*arrays)
        return line_body(planes, heads, *arrays)

    in_specs = (
        P("batch", None, "head"),
        P("batch", "head"),
        P("batch", "head"),
        P("batch", "head"),
        P("batch", "head"),
        P("head", "batch"),
        P("batch", None, None),
        P("batch", "head", None, None),
    )
    out_specs = (P("batch", None, "head"), P("batch", "head", None, None))
    return jax.shard_map(body, mesh=mesh, in_specs=in_specs, out_specs=out_specs, check_vma=False)
```

```python
import functools

import jax
import jax.numpy as jnp
from jax import lax
from jax.experimental import pallas as pl
from jax.experimental.pallas import tpu as pltpu
from jax.sharding import PartitionSpec as P

SEGS = 2
CORES = 2
PAD = 8
epsilon = 1e-05


def recur(query, keys, values, beta, state):
    highest = lax.Precision.HIGHEST
    readouts = []
    for segment in range(query.shape[1]):
        readouts.append(
            jnp.einsum("bhij,blhj->blhi", state, query[:, segment], precision=highest).astype(
                jnp.bfloat16
            )
        )
        recalled = jnp.einsum("bhij,bmhj->bmhi", state, keys[:, segment], precision=highest)
        change = beta[:, segment][..., None] * (values[:, segment] - recalled)
        state = state + jnp.einsum("bmhi,bmhj->bhij", change, keys[:, segment], precision=highest)
    return (jnp.stack(readouts, axis=1), state)


def general_body(hidden_in, w_query, w_key, w_value, w_beta, w_out, mem_pos, memory_in):
    seq_count, row_count, local_width = hidden_in.shape
    seg_rows = row_count // SEGS
    mem_count = mem_pos.shape[2]
    local_heads = w_beta.shape[1]
    local_features = w_query.shape[1]
    head_size = local_features // local_heads
    x_float = hidden_in.astype(jnp.float32)
    whole = lax.all_gather(hidden_in, "head", axis=2, tiled=True)
    whole_float = whole.astype(jnp.float32)
    mean_square = jnp.mean(whole_float * whole_float, axis=2, keepdims=True)
    normed = (whole_float * lax.rsqrt(mean_square + epsilon)).astype(jnp.bfloat16)
    full_width = normed.shape[2]
    offsets = (jnp.arange(SEGS, dtype=jnp.int32) * seg_rows)[None, :, None]
    picked = (mem_pos + offsets).reshape(seq_count, SEGS * mem_count)
    memory_rows = jax.vmap(lambda block, where: jnp.take(block, where, axis=0))(normed, picked)
    memory_rows = memory_rows.reshape(seq_count * SEGS * mem_count, full_width)
    token_rows = normed.reshape(seq_count * row_count, full_width)
    piece_query = lax.all_gather(w_query, "batch", axis=0, tiled=True)
    piece_key = lax.all_gather(w_key, "batch", axis=0, tiled=True)
    piece_value = lax.all_gather(w_value, "batch", axis=0, tiled=True)
    piece_beta = lax.all_gather(w_beta, "batch", axis=0, tiled=True)
    query = jnp.dot(token_rows, piece_query, preferred_element_type=jnp.float32)
    keys = jnp.dot(memory_rows, piece_key, preferred_element_type=jnp.float32)
    values = jnp.dot(memory_rows, piece_value, preferred_element_type=jnp.float32)
    logits = jnp.dot(memory_rows, piece_beta, preferred_element_type=jnp.float32)
    query = (query * head_size ** (-0.5)).reshape(seq_count, SEGS, seg_rows, local_heads, head_size)
    keys = keys.reshape(seq_count, SEGS, mem_count, local_heads, head_size)
    keys = keys * lax.rsqrt(jnp.sum(keys * keys, axis=-1, keepdims=True) + 1e-06)
    values = values.reshape(seq_count, SEGS, mem_count, local_heads, head_size)
    beta = jax.nn.sigmoid(logits).reshape(seq_count, SEGS, mem_count, local_heads)
    readout, state = recur(query, keys, values, beta, memory_in)
    readout = readout.reshape(seq_count * row_count, local_features)
    terms = jnp.dot(
        readout,
        lax.all_gather(w_out, "batch", axis=1, tiled=True),
        preferred_element_type=jnp.float32,
    )
    mixed = lax.psum_scatter(terms, "head", scatter_dimension=1, tiled=True)
    hidden_out = (mixed + x_float.reshape(seq_count * row_count, local_width)).astype(jnp.bfloat16)
    return (hidden_out.reshape(hidden_in.shape), state)


VM = pl.BlockSpec(memory_space=pltpu.VMEM)
SM = pl.BlockSpec(memory_space=pltpu.SMEM)


def call(kernel, args, outs, scratch=(), flops=0, grid=(), specs=None, out_specs=None, room=24):
    size = sum(a.size * a.dtype.itemsize for a in list(args[1:]) + list(outs))
    return pl.pallas_call(
        kernel,
        out_shape=outs,
        grid=grid,
        in_specs=[SM] + list(specs or [VM] * (len(args) - 1)),
        out_specs=list(out_specs or [VM] * len(outs)),
        scratch_shapes=list(scratch),
        compiler_params=pltpu.CompilerParams(vmem_limit_bytes=room << 20),
        cost_estimate=pl.CostEstimate(flops=flops, bytes_accessed=size, transcendentals=0),
    )(*args)


def whole(value):
    return pl.BlockSpec(value.shape, lambda n: (0,) * len(value.shape))


def columns_of(value, tile):
    return pl.BlockSpec((value.shape[0], tile), lambda n: (0, n))


def norm_kernel(heads, width, ids, *refs):
    blocks = refs[:heads]
    places = refs[heads]
    outs = refs[heads + 1 : -1]
    held = refs[-1]
    square = None
    for block in blocks:
        value = block[...].astype(jnp.float32)
        part = jnp.sum(value * value, axis=-1, keepdims=True)
        square = part if square is None else square + part
    scale = lax.rsqrt(square / width + epsilon)
    for m, block in enumerate(blocks):
        held[m] = (block[...].astype(jnp.float32) * scale).astype(jnp.bfloat16)
    mix = ids[0] ^ ids[1]
    rows, mem = held.shape[2], places.shape[1]
    for s in range(SEGS):
        for j in range(heads):
            out = outs[s * heads + j]
            out[:rows, :] = held[mix ^ j, s]
            if s == 0:
                out[rows:, :] = jnp.zeros((PAD, out.shape[1]), jnp.bfloat16)
                shown = places[...].astype(jnp.float32).astype(jnp.bfloat16)
                out[rows : rows + SEGS, :mem] = shown


def gather_pieces(heads, ids, pieces, rows):
    piece = pieces[0].shape[1]
    for m in range(heads):
        start = pl.multiple_of((ids[0] ^ m) * piece, piece)
        for j in range(heads):
            rows[j, pl.ds(start, piece), :] = pieces[m][j]


def weight_rows(ids, depth):
    mine = pl.ds(pl.multiple_of(ids[2] * depth, depth), depth)
    theirs = pl.ds(pl.multiple_of((1 - ids[2]) * depth, depth), depth)
    return mine, theirs


def product(source, parts, own, other):
    depth = own.shape[0]
    mine, theirs = parts
    return (
        jnp.dot(
            source[:, :, mine].reshape(-1, depth), own[...], preferred_element_type=jnp.float32
        )
        + jnp.dot(
            source[:, :, theirs].reshape(-1, depth), other[...], preferred_element_type=jnp.float32
        )
    ).astype(jnp.bfloat16)


def query_kernel(heads, ids, *refs):
    pieces = refs[:heads]
    own, other = refs[heads : heads + 2]
    outs = refs[heads + 2 : -1]
    rows = refs[-1]

    @pl.when(pl.program_id(0) == 0)
    def _():
        gather_pieces(heads, ids, pieces, rows)

    result = product(rows, weight_rows(ids, own.shape[0]), own, other)
    count = rows.shape[1]
    for j in range(heads):
        outs[j][...] = result[j * count : (j + 1) * count]


def project_kernel(heads, mem, size, ids, *refs):
    pieces = [refs[:heads], refs[heads : 2 * heads]]
    pos = refs[2 * heads : 3 * heads]
    own = refs[3 * heads : 3 * heads + 4]
    other = refs[3 * heads + 4 : 3 * heads + 8]
    outs = refs[3 * heads + 8 : -4]
    first, rows, picked, logits = refs[-4:]
    seg_rows = rows.shape[1]
    piece = pieces[0][0].shape[1]
    parts = weight_rows(ids, own[0].shape[0])
    n = pl.program_id(0)

    @pl.when(n == 0)
    def _():
        token = lax.broadcasted_iota(jnp.int32, (seg_rows, mem), 0).astype(jnp.float32)
        contract = (((1,), (1,)), ((), ()))
        for s, source in enumerate((first, rows)):
            gather_pieces(heads, ids, pieces[s], source)
            for j in range(heads):
                where = pos[j][piece:, :][s : s + 1, :mem].astype(jnp.float32)
                hot = jnp.where(token == where, 1.0, 0.0).astype(jnp.bfloat16)
                chosen = lax.dot_general(
                    hot, source[j], (((0,), (0,)), ((), ())), preferred_element_type=jnp.float32
                ).astype(jnp.bfloat16)
                picked[s * heads + j] = chosen
                logits[s * heads + j] = sum(
                    lax.dot_general(
                        weight[...],
                        picked[s * heads + j, :, part],
                        contract,
                        preferred_element_type=jnp.float32,
                    )
                    for weight, part in ((own[3], parts[0]), (other[3], parts[1]))
                )

    query = product(rows, parts, own[0], other[0])
    pairs = [product(picked, parts, own[kind], other[kind]) for kind in (1, 2)]
    tile = own[0].shape[1]
    for j in range(heads):
        outs[j][:seg_rows, :] = query[j * seg_rows : (j + 1) * seg_rows]
    for index in range(SEGS * heads):
        out = outs[index]
        top = seg_rows if index < heads else 0
        for result in pairs:
            out[top : top + mem, :] = result[index * mem : (index + 1) * mem]
            top += mem
        for k in range(tile // size):
            logit = logits[index, pl.ds(n * (tile // size) + k, 1), :]
            shown = jnp.broadcast_to(logit, (PAD, mem)).astype(jnp.bfloat16)
            out[top:, k * size : k * size + mem] = shown
            out[top:, k * size + mem : (k + 1) * size] = jnp.zeros(
                (PAD, size - mem), jnp.bfloat16
            )


HIGHEST = lax.Precision.HIGHEST
ACROSS = (((1,), (1,)), ((), ()))


def summed(parts, held):
    value = parts[0][...].astype(jnp.float32)
    for part in parts[1:]:
        value = value + part[...].astype(jnp.float32)
    held[...] = value


def read_states(held, states, readout, seg_rows):
    size = readout.shape[1] // len(states)
    for head, state in enumerate(states):
        columns = slice(head * size, (head + 1) * size)
        query = held[:seg_rows, columns] * size ** (-0.5)
        readout[:, columns] = lax.dot_general(
            query, state, ACROSS, precision=HIGHEST, preferred_element_type=jnp.float32
        ).astype(jnp.bfloat16)


def update_states(held, states, state_out, first, mem_rows):
    size = states[0].shape[-1]
    kept = []
    for head, state in enumerate(states):
        columns = slice(head * size, (head + 1) * size)
        keys = held[first : first + mem_rows, columns]
        keys = keys * lax.rsqrt(jnp.sum(keys * keys, axis=-1, keepdims=True) + 1e-06)
        recalled = lax.dot_general(
            keys, state, ACROSS, precision=HIGHEST, preferred_element_type=jnp.float32
        )
        kept.append((keys, recalled))
    changes = []
    for head, (keys, recalled) in enumerate(kept):
        columns = slice(head * size, (head + 1) * size)
        values = held[first + mem_rows : first + 2 * mem_rows, columns]
        logits = held[first + 2 * mem_rows :, columns]
        beta = jax.nn.sigmoid(logits).T[:mem_rows, :1]
        changes.append(beta * (values - recalled))
    later = []
    for head, state in enumerate(states):
        later.append(
            state
            + lax.dot_general(
                changes[head],
                kept[head][0],
                (((0,), (0,)), ((), ())),
                precision=HIGHEST,
                preferred_element_type=jnp.float32,
            )
        )
        state_out[head] = later[head]
    return later


def heads_in(state_in):
    return [state_in[head] for head in range(state_in.shape[0])]


def both_kernel(count, seg_rows, mem_rows, ids, *refs):
    state_in, readout, state_out, held = refs[count:]
    summed(refs[:count], held)
    states = update_states(held, heads_in(state_in), state_out, seg_rows, mem_rows)
    read_states(held, states, readout, seg_rows)


def read_kernel(count, seg_rows, ids, *refs):
    state_in, readout, held = refs[count:]
    summed(refs[:count], held)
    read_states(held, heads_in(state_in), readout, seg_rows)


def update_kernel(count, mem_rows, ids, *refs):
    state_in, state_out, held = refs[count:]
    summed(refs[:count], held)
    update_states(held, heads_in(state_in), state_out, 0, mem_rows)


def out_kernel(heads, ids, *refs):
    readout = refs[0]
    own = refs[1 : 1 + heads]
    other = refs[1 + heads : 1 + 2 * heads]
    outs = refs[1 + 2 * heads : 1 + 3 * heads]
    held = refs[-1]
    tile = own[0].shape[1]
    n = pl.program_id(0)
    steps = pl.num_programs(0)
    mix = ids[0] ^ ids[1]
    rows = readout[...]
    for j in range(heads):
        for core, weights in ((ids[2], own[j]), (1 - ids[2], other[j])):
            start = pl.multiple_of((core * steps + n) * tile, tile)
            held[mix ^ j, :, pl.ds(start, tile)] = jnp.dot(
                rows, weights[...], preferred_element_type=jnp.float32
            )

    @pl.when(n == steps - 1)
    def _():
        for m in range(heads):
            outs[m][...] = held[m].astype(outs[m].dtype)


def line_body(planes, heads, *arrays):
    hidden_in, w_query, w_key, w_value, w_beta, w_out, mem_pos, memory_in = arrays
    row_count, width = hidden_in.shape[1:]
    seg_rows, mem_rows = row_count // SEGS, mem_pos.shape[2]
    piece = seg_rows // heads
    local_heads = w_beta.shape[1]
    features = w_query.shape[1]
    full_width = width * heads
    size = features // local_heads
    tile = min(256, features)
    bf16, f32 = jnp.bfloat16, jnp.float32
    h, b = lax.axis_index("head"), lax.axis_index("batch")
    z, core = b // CORES, b % CORES
    ids = jnp.stack([h, z, core]).astype(jnp.int32)
    shape = jax.ShapeDtypeStruct

    def over_head(value, m):
        return lax.ppermute(value, "head", [(i, i ^ m) for i in range(heads)])

    def over_z(value, j):
        pairs = [(i, i ^ (j * CORES)) for i in range(planes * CORES)]
        return lax.ppermute(value, "batch", pairs)

    def over_core(value):
        return lax.ppermute(value, "batch", [(i, i ^ 1) for i in range(planes * CORES)])

    def edge(value, i):
        pairs = []
        for c in range(CORES):
            pairs.append((i * CORES + c, (i + 1) * CORES + c))
            pairs.append(((planes - 1 - i) * CORES + c, (planes - 2 - i) * CORES + c))
        return lax.ppermute(value, "batch", pairs)

    middle = w_out.shape[0] // 2
    halves = [w_out[:middle]]
    x = hidden_in.reshape(SEGS, heads, piece, width)
    quarter = lambda m: lax.dynamic_index_in_dim(x, h ^ m, axis=1, keepdims=False)
    blocks = [quarter(0)] + [over_head(quarter(m), m) for m in range(1, heads)]
    weights = [w_query, w_key, w_value, w_beta.T]
    partner = [over_core(w) for w in weights]
    normed = call(
        functools.partial(norm_kernel, heads, full_width),
        [ids] + blocks + [mem_pos[0]],
        [shape((piece + PAD, width), bf16)] * planes + [shape((piece, width), bf16)] * planes,
        [pltpu.VMEM((heads, SEGS, piece, width), bf16)],
        room=8,
    )
    halves.append(lax.optimization_barrier((w_out, normed[0]))[0][middle:])
    near = [over_z(half, 1) for half in halves]
    across = [edge(half, 1) for half in halves]
    from_near = [edge(half, 1) for half in near]
    outward = [edge(half, 2) for half in across]
    farthest = [edge(half, 2) for half in from_near]
    pieces = []
    for s in range(SEGS):
        mine = normed[s * planes : (s + 1) * planes]
        got = [mine[0]] + [over_z(mine[j], j) for j in range(1, planes)]
        if s == 0:
            pos = got
        held = jnp.stack([value[:piece] for value in got])
        pieces.append([held] + [over_head(held, m) for m in range(1, heads)])
    tiles = lambda values: [columns_of(v, tile) for v in values]
    column_tile = lambda count: pl.BlockSpec((count, tile), lambda n: (0, n))
    queries = call(
        functools.partial(query_kernel, heads),
        [ids] + pieces[0] + [w_query, partner[0]],
        [shape((seg_rows, features), bf16)] * planes,
        [pltpu.VMEM((planes, seg_rows, width), bf16)],
        flops=2 * planes * width * features * seg_rows,
        room=16,
        grid=(features // tile,),
        specs=[whole(v) for v in pieces[0]] + tiles([w_query, partner[0]]),
        out_specs=[column_tile(seg_rows)] * planes,
    )
    few = 2 * mem_rows + PAD
    counts = [seg_rows + few] * planes + [few] * planes
    products = call(
        functools.partial(project_kernel, heads, mem_rows, size),
        [ids] + pieces[0] + pieces[1] + pos + weights + partner,
        [shape((count, features), bf16) for count in counts],
        [
            pltpu.VMEM((planes, seg_rows, width), bf16),
            pltpu.VMEM((planes, seg_rows, width), bf16),
            pltpu.VMEM((SEGS * planes, mem_rows, width), bf16),
            pltpu.VMEM((SEGS * planes, local_heads, mem_rows), f32),
        ],
        flops=2 * planes * width * features * (seg_rows + 4 * mem_rows),
        grid=(features // tile,),
        specs=[whole(v) for v in pieces[0] + pieces[1] + pos]
        + tiles(weights[:3])
        + [whole(weights[3])]
        + tiles(partner[:3])
        + [whole(weights[3])],
        out_specs=[column_tile(count) for count in counts],
    )
    outer = (z == 0) | (z == planes - 1)
    rows_of = lambda parts: jnp.concatenate(parts, axis=0)
    y = [
        w_out,
        rows_of(near),
        jnp.where(outer, rows_of(outward), rows_of(from_near)),
        jnp.where(outer, rows_of(farthest), rows_of(across)),
    ]
    y_partner = [over_core(v) for v in y]
    add = lambda a, c: (a.astype(f32) + c.astype(f32)).astype(bf16)

    def line_sum(u):
        t03 = edge(u[3], 0)
        t02 = edge(u[2], 0)
        t13 = edge(add(u[2], t03), 1)
        t12 = edge(add(u[3], t02), 1)
        pair = over_z(add(u[1], t13), 1)
        return [u[0], pair, t12]

    read_shape = shape((seg_rows, features), bf16)
    state_shape = shape(memory_in.shape[1:], f32)

    def emit(readout, s):
        mixed = call(
            functools.partial(out_kernel, heads),
            [ids, readout] + y + y_partner,
            [shape((seg_rows, width), f32)] + [shape((seg_rows, width), bf16)] * (heads - 1),
            [pltpu.VMEM((heads, seg_rows, width), f32)],
            flops=2 * seg_rows * features * full_width,
            grid=(w_out.shape[1] // tile,),
            specs=[whole(readout)] + [columns_of(v, tile) for v in y + y_partner],
            out_specs=[pl.BlockSpec((seg_rows, width), lambda n: (0, 0))] * heads,
        )
        total = mixed[0]
        for m in range(1, heads):
            total = total + over_head(mixed[m], m).astype(f32)
        rows = hidden_in[0, s * seg_rows : (s + 1) * seg_rows].astype(f32)
        return (total + rows).astype(bf16)

    state = memory_in[0]
    sums = line_sum(queries)
    readout = call(
        functools.partial(read_kernel, 3, seg_rows),
        [ids] + sums + [state],
        [read_shape],
        room=8,
        scratch=[pltpu.VMEM(sums[0].shape, f32)],
    )[0]
    outs = [emit(readout, 0)]
    sums = line_sum(products[:planes])
    readout, state = call(
        functools.partial(both_kernel, 3, seg_rows, mem_rows),
        [ids] + sums + [state],
        [read_shape, state_shape],
        room=12,
        scratch=[pltpu.VMEM(sums[0].shape, f32)],
    )
    outs.append(emit(readout, 1))
    sums = line_sum(products[planes:])
    state = call(
        functools.partial(update_kernel, 3, mem_rows),
        [ids] + sums + [state],
        [state_shape],
        room=8,
        scratch=[pltpu.VMEM(sums[0].shape, f32)],
    )[0]
    return (jnp.concatenate(outs, axis=0)[None], state[None])


def solution(mesh):
    heads, batch = mesh.shape["head"], mesh.shape["batch"]
    planes = batch // CORES
    lined = planes == heads == 4

    def body(*arrays):
        if not lined:
            return general_body(*arrays)
        return line_body(planes, heads, *arrays)

    in_specs = (
        P("batch", None, "head"),
        P("batch", "head"),
        P("batch", "head"),
        P("batch", "head"),
        P("batch", "head"),
        P("head", "batch"),
        P("batch", None, None),
        P("batch", "head", None, None),
    )
    out_specs = (P("batch", None, "head"), P("batch", "head", None, None))
    return jax.shard_map(body, mesh=mesh, in_specs=in_specs, out_specs=out_specs, check_vma=False)
```
